32 devices in a mesh: replica: 8 (over y, x, core), shard: 4 (over z).
Axes of the slice: x: 2, y: 2, z: 4, core: 2. Of those that a mesh axis runs over, the one named last changes fastest.
Arguments:
- inputs: float32 [32, 128, 960], P(('replica', 'shard')), may hold values from -6 to 6
- cotangent: float32 [32, 128, 960], P(('replica', 'shard')), may hold values from -6 to 6
- w_query: float32 [960, 960], P('shard', 'replica'), may hold values from -0.1875 to 0.1875
- w_key: float32 [960, 320], P('shard', 'replica'), may hold values from -0.1875 to 0.1875
- w_value: float32 [960, 320], P('shard', 'replica'), may hold values from -0.1875 to 0.1875
- w_merge: float32 [960, 960], P('shard', 'replica'), may hold values from -0.5 to 0.5
- w_gate: float32 [960, 2560], P('shard', 'replica'), may hold values from -0.1875 to 0.1875
- w_up: float32 [960, 2560], P('shard', 'replica'), may hold values from -0.1875 to 0.1875
- w_down: float32 [2560, 960], P('shard', 'replica'), may hold values from -0.125 to 0.125
- gain_attn: float32 [960], P('shard'), may hold values from 0.5 to 1.5
- gain_mlp: float32 [960], P('shard'), may hold values from 0.5 to 1.5
- mom_query: float32 [2, 960, 960], P(None, 'shard', 'replica'), as said below
- mom_key: float32 [2, 960, 320], P(None, 'shard', 'replica'), as said below
- mom_value: float32 [2, 960, 320], P(None, 'shard', 'replica'), as said below
- mom_merge: float32 [2, 960, 960], P(None, 'shard', 'replica'), as said below
- mom_gate: float32 [2, 960, 2560], P(None, 'shard', 'replica'), as said below
- mom_up: float32 [2, 960, 2560], P(None, 'shard', 'replica'), as said below
- mom_down: float32 [2, 2560, 960], P(None, 'shard', 'replica'), as said below
- mom_attn: float32 [2, 960], P(None, 'shard'), as said below
- mom_mlp: float32 [2, 960], P(None, 'shard'), as said below
Outputs:
- output: float32 [32, 128, 960], P(('replica', 'shard'))
- input_grad: float32 [32, 128, 960], P(('replica', 'shard'))
- grad_query: float32 [960, 960], P('shard', 'replica')
- grad_key: float32 [960, 320], P('shard', 'replica')
- grad_value: float32 [960, 320], P('shard', 'replica')
- grad_merge: float32 [960, 960], P('shard', 'replica')
- grad_gate: float32 [960, 2560], P('shard', 'replica')
- grad_up: float32 [960, 2560], P('shard', 'replica')
- grad_down: float32 [2560, 960], P('shard', 'replica')
- grad_attn: float32 [960], P('shard')
- grad_mlp: float32 [960], P('shard')
- new_query: float32 [960, 960], P('shard', 'replica')
- new_key: float32 [960, 320], P('shard', 'replica')
- new_value: float32 [960, 320], P('shard', 'replica')
- new_merge: float32 [960, 960], P('shard', 'replica')
- new_gate: float32 [960, 2560], P('shard', 'replica')
- new_up: float32 [960, 2560], P('shard', 'replica')
- new_down: float32 [2560, 960], P('shard', 'replica')
- new_attn: float32 [960], P('shard')
- new_mlp: float32 [960], P('shard')
- next_query: float32 [2, 960, 960], P(None, 'shard', 'replica')
- next_key: float32 [2, 960, 320], P(None, 'shard', 'replica')
- next_value: float32 [2, 960, 320], P(None, 'shard', 'replica')
- next_merge: float32 [2, 960, 960], P(None, 'shard', 'replica')
- next_gate: float32 [2, 960, 2560], P(None, 'shard', 'replica')
- next_up: float32 [2, 960, 2560], P(None, 'shard', 'replica')
- next_down: float32 [2, 2560, 960], P(None, 'shard', 'replica')
- next_attn: float32 [2, 960], P(None, 'shard')
- next_mlp: float32 [2, 960], P(None, 'shard')
The draws below stay inside these ranges and needn't reach their ends.
Inputs may be any that keep to these rules, and one draw needn't show every extreme that they name: `mom_query`: the second of the two stacked moments is positive. `mom_key`: the second of the two stacked moments is positive. `mom_value`: the second of the two stacked moments is positive. `mom_merge`: the second of the two stacked moments is positive. `mom_gate`: the second of the two stacked moments is positive. `mom_up`: the second of the two stacked moments is positive. `mom_down`: the second of the two stacked moments is positive. `mom_attn`: the second of the two stacked moments is positive. `mom_mlp`: the second of the two stacked moments is positive.
All inputs are finite; a program needn't handle non-finite values.
Results may differ from the reference program's by a relative error of at most 0.018.
Values may be sent and summed in bfloat16 or wider, within the bound.
No kernel may reach another device: no remote copies, remote signals or barrier semaphores. Data moves between devices by JAX's collectives and lax.ppermute only.
A program may use at most 128 MiB of HBM per device.

```python
import math
import jax
import jax.numpy as jnp
from jax import lax

D = 960
H = 15
KV = 5
HEAD = 64
FF = 2560
SEQ_LEN = 128
SEQS = 32
TOKENS = 4096
QW = 960
KVW = 320


def moment_pair(key, shape, label, grad_size):
    first_moment = 0.5 * grad_size * jnp.clip(jax.random.normal(jax.random.fold_in(key, label), shape, jnp.float32), -4.0, 4.0)
    ratio = 0.05 / 0.95
    factor = jnp.exp(jax.random.uniform(jax.random.fold_in(key, label + 100), shape, jnp.float32, math.log(0.5), math.log(8.0)))
    second = ratio * grad_size * grad_size * factor
    return jnp.stack([first_moment, second])


def draw_mom_query(key, part):
    return moment_pair(key, (D, H * HEAD), 31, 0.1)


def draw_mom_key(key, part):
    return moment_pair(key, (D, KV * HEAD), 32, 0.1)


def draw_mom_value(key, part):
    return moment_pair(key, (D, KV * HEAD), 33, 0.2)


def draw_mom_merge(key, part):
    return moment_pair(key, (H * HEAD, D), 34, 0.3)


def draw_mom_gate(key, part):
    return moment_pair(key, (D, FF), 35, 0.5 * math.sqrt(D / FF))


def draw_mom_up(key, part):
    return moment_pair(key, (D, FF), 36, 0.5 * math.sqrt(D / FF))


def draw_mom_down(key, part):
    return moment_pair(key, (FF, D), 37, 0.5)


def draw_mom_attn(key, part):
    return moment_pair(key, (D,), 38, 0.5)


def draw_mom_mlp(key, part):
    return moment_pair(key, (D,), 39, 0.5)


def level_of(own_key, extent, cuts, least, largest):
    factor_of = 1.0
    for position, parts in cuts:
        heights = jax.random.uniform(jax.random.fold_in(jax.random.fold_in(own_key, 6), position), (parts,), jnp.float32, least / len(cuts), largest / len(cuts))
        factor_of = factor_of * jnp.repeat(jnp.exp(heights), extent[position] // parts).reshape((-1,) + (1,) * (len(extent) - 1 - position))
    return factor_of


def gaussian(stream_key, shape, width, limit, shards=(), kind=jnp.bfloat16):
    level = level_of(stream_key, shape, shards, -0.22, 0.18) if shards else 1.0
    drawn = jax.random.normal(stream_key, shape, jnp.float32) * width * level
    return jnp.minimum(jnp.maximum(drawn, -limit), limit).astype(kind)


def setup_inputs(seed: int = 0) -> dict:
    keys = jax.random.split(jax.random.key(seed), 21)
    return {
        "inputs": gaussian(keys[0], (SEQS, SEQ_LEN, D), 1.0, 6.0, ((0, 32),), jnp.float32),
        "cotangent": gaussian(keys[1], (SEQS, SEQ_LEN, D), 1.0, 6.0, ((0, 32),), jnp.float32),
        "w_query": gaussian(keys[2], (D, QW), D ** -0.5, 0.1875, ((0, 4), (1, 8)), jnp.float32),
        "w_key": gaussian(keys[3], (D, KVW), D ** -0.5, 0.1875, ((0, 4), (1, 8)), jnp.float32),
        "w_value": gaussian(keys[4], (D, KVW), D ** -0.5, 0.1875, ((0, 4), (1, 8)), jnp.float32),
        "w_merge": gaussian(keys[5], (QW, D), (QW // 8) ** -0.5, 0.5, ((0, 4), (1, 8)), jnp.float32),
        "w_gate": gaussian(keys[6], (D, FF), D ** -0.5, 0.1875, ((0, 4), (1, 8)), jnp.float32),
        "w_up": gaussian(keys[7], (D, FF), D ** -0.5, 0.1875, ((0, 4), (1, 8)), jnp.float32),
        "w_down": gaussian(keys[8], (FF, D), FF ** -0.5, 0.125, ((0, 4), (1, 8)), jnp.float32),
        "gain_attn": jnp.clip(1.0 + 0.1 * jax.random.normal(keys[9], (D,), jnp.float32), 0.5, 1.5),
        "gain_mlp": jnp.clip(1.0 + 0.1 * jax.random.normal(keys[10], (D,), jnp.float32), 0.5, 1.5),
        "mom_query": draw_mom_query(jax.random.fold_in(keys[20], 71), 0),
        "mom_key": draw_mom_key(jax.random.fold_in(keys[20], 71), 0),
        "mom_value": draw_mom_value(jax.random.fold_in(keys[20], 71), 0),
        "mom_merge": draw_mom_merge(jax.random.fold_in(keys[20], 71), 0),
        "mom_gate": draw_mom_gate(jax.random.fold_in(keys[20], 71), 0),
        "mom_up": draw_mom_up(jax.random.fold_in(keys[20], 71), 0),
        "mom_down": draw_mom_down(jax.random.fold_in(keys[20], 71), 0),
        "mom_attn": draw_mom_attn(jax.random.fold_in(keys[20], 71), 0),
        "mom_mlp": draw_mom_mlp(jax.random.fold_in(keys[20], 71), 0),
    }


EPS_NORM = 1e-05
THETA = 100000.0
BETA_ONE = 0.9
BETA_TWO = 0.95
ADAM_EPS = 1e-08
LEARN_RATE = 0.01
GAIN_RATE = 0.1
WEIGHT_DECAY = 0.1
STEP_COUNT = 3.0
NEG_LARGE = -1e+30

def rotary_tables(seq_len, head_dim):
    half_head = head_dim // 2
    frequency = THETA ** (-2.0 * jnp.arange(half_head, dtype=jnp.float32) / head_dim)
    angles = jnp.arange(seq_len, dtype=jnp.float32)[:, None] * frequency[None, :]
    angles = jnp.concatenate([angles, angles], axis=1)
    return (jnp.cos(angles), jnp.sin(angles))

def rotate(values, cosine_table, sine_table):
    half_head = values.shape[-1] // 2
    turned = jnp.concatenate([-values[..., half_head:], values[..., :half_head]], axis=-1)
    return values * cosine_table[None, :, None, :] + turned * sine_table[None, :, None, :]

def unrotate(grads, cosine_table, sine_table):
    half_head = grads.shape[-1] // 2
    scaled = grads * sine_table[None, :, None, :]
    turned = jnp.concatenate([scaled[..., half_head:], -scaled[..., :half_head]], axis=-1)
    return grads * cosine_table[None, :, None, :] + turned

def matmul(left_side, right_side):
    return jnp.dot(left_side, right_side, preferred_element_type=jnp.float32)

def norm_forward(field, gain_half):
    reciprocal = lax.rsqrt(lax.optimization_barrier(jnp.mean(field * field, axis=-1, keepdims=True)) + EPS_NORM)
    unit_field = field * reciprocal
    return (unit_field, reciprocal, (unit_field * gain_half.astype(jnp.float32)).astype(jnp.bfloat16))

def norm_backward(grad_normed, unit_field, reciprocal, gain_half):
    gain_sum = lax.optimization_barrier(jnp.sum(grad_normed * unit_field, axis=0))
    grad_unit = grad_normed * gain_half.astype(jnp.float32)
    grad_field = reciprocal * (grad_unit - unit_field * lax.optimization_barrier(jnp.mean(grad_unit * unit_field, axis=-1, keepdims=True)))
    return (grad_field, gain_sum)

def attend(queries, key_rows, values):
    count_seqs, seq_len, num_heads, head_dim = queries.shape
    kv_heads = key_rows.shape[2]
    group_size = num_heads // kv_heads
    grouped = queries.astype(jnp.float32).reshape(count_seqs, seq_len, kv_heads, group_size, head_dim)
    scores = jnp.einsum('bqkgd,bskd->bkgqs', grouped, key_rows.astype(jnp.float32)) / math.sqrt(head_dim)
    causal = jnp.arange(seq_len)[:, None] >= jnp.arange(seq_len)[None, :]
    scores = jnp.where(causal, scores, NEG_LARGE)
    row_max = lax.optimization_barrier(jnp.max(scores, axis=-1, keepdims=True))
    log_total = row_max + jnp.log(lax.optimization_barrier(jnp.sum(jnp.exp(scores - row_max), axis=-1, keepdims=True)))
    attn_prob = jnp.exp(scores - log_total).astype(jnp.bfloat16)
    mixed_heads = jnp.einsum('bkgqs,bskd->bqkgd', attn_prob.astype(jnp.float32), values.astype(jnp.float32))
    return (mixed_heads.reshape(count_seqs * seq_len, num_heads * head_dim).astype(jnp.bfloat16), log_total)

def attend_back(queries, key_rows, values, log_total, grad_heads):
    count_seqs, seq_len, num_heads, head_dim = queries.shape
    kv_heads = key_rows.shape[2]
    group_size = num_heads // kv_heads
    grouped = queries.astype(jnp.float32).reshape(count_seqs, seq_len, kv_heads, group_size, head_dim)
    key_full = key_rows.astype(jnp.float32)
    scores = jnp.einsum('bqkgd,bskd->bkgqs', grouped, key_full) / math.sqrt(head_dim)
    causal = jnp.arange(seq_len)[:, None] >= jnp.arange(seq_len)[None, :]
    scores = jnp.where(causal, scores, NEG_LARGE)
    probs_full = jnp.exp(scores - log_total)
    attn_prob = probs_full.astype(jnp.bfloat16).astype(jnp.float32)
    grad_grouped = grad_heads.astype(jnp.float32).reshape(count_seqs, seq_len, kv_heads, group_size, head_dim)
    grad_prob = jnp.einsum('bqkgd,bskd->bkgqs', grad_grouped, values.astype(jnp.float32))
    grad_values = jnp.einsum('bkgqs,bqkgd->bskd', attn_prob, grad_grouped)
    grad_scores = probs_full * (grad_prob - lax.optimization_barrier(jnp.sum(probs_full * grad_prob, axis=-1, keepdims=True)))
    grad_scores = (grad_scores / math.sqrt(head_dim)).astype(jnp.bfloat16).astype(jnp.float32)
    grad_queries = jnp.einsum('bkgqs,bskd->bqkgd', grad_scores, key_full).reshape(count_seqs, seq_len, num_heads, head_dim)
    grad_keys = jnp.einsum('bkgqs,bqkgd->bskd', grad_scores, grouped)
    return (grad_queries, grad_keys, grad_values)

def forward_pass(inputs, weights, gains, cosine_table, sine_table):
    w_query, w_key, w_value, w_merge, w_gate, w_up, w_down = weights
    count_seqs, seq_len, model_width = inputs.shape
    flat_in = inputs.reshape(count_seqs * seq_len, model_width)
    unit_one, recip_one, normed_one = norm_forward(flat_in, gains[0])
    queries = rotate(matmul(normed_one, w_query).reshape(count_seqs, seq_len, H, HEAD), cosine_table, sine_table).astype(jnp.bfloat16)
    key_rows = rotate(matmul(normed_one, w_key).reshape(count_seqs, seq_len, KV, HEAD), cosine_table, sine_table).astype(jnp.bfloat16)
    values = matmul(normed_one, w_value).astype(jnp.bfloat16).reshape(count_seqs, seq_len, KV, HEAD)
    mixed_heads, log_total = attend(queries, key_rows, values)
    middle = flat_in + matmul(mixed_heads, w_merge)
    unit_two, recip_two, normed_two = norm_forward(middle, gains[1])
    gate_pre = matmul(normed_two, w_gate)
    up_value = matmul(normed_two, w_up)
    hidden = (jax.nn.silu(gate_pre) * up_value).astype(jnp.bfloat16)
    output = middle + matmul(hidden, w_down)
    saved = (unit_one, recip_one, normed_one, queries, key_rows, values, log_total, mixed_heads, unit_two, recip_two, normed_two, gate_pre, up_value, hidden)
    return (output.reshape(inputs.shape), saved)

def backward_pass(cotangent, saved, weights, gains, cosine_table, sine_table):
    w_query, w_key, w_value, w_merge, w_gate, w_up, w_down = weights
    unit_one, recip_one, normed_one, queries, key_rows, values, log_total, mixed_heads, unit_two, recip_two, normed_two, gate_pre, up_value, hidden = saved
    count_seqs, seq_len, model_width = cotangent.shape
    flat_cot = cotangent.reshape(count_seqs * seq_len, model_width)
    grad_out16 = flat_cot.astype(jnp.bfloat16)
    grad_wdown = matmul(hidden.T, grad_out16)
    grad_hidden = matmul(grad_out16, w_down.T)
    sigmoid_gate = jax.nn.sigmoid(gate_pre)
    grad_up16 = (grad_hidden * gate_pre * sigmoid_gate).astype(jnp.bfloat16)
    grad_gate16 = (grad_hidden * up_value * sigmoid_gate * (1.0 + gate_pre * (1.0 - sigmoid_gate))).astype(jnp.bfloat16)
    grad_wgate = matmul(normed_two.T, grad_gate16)
    grad_wup = matmul(normed_two.T, grad_up16)
    grad_normed_two = matmul(grad_gate16, w_gate.T) + matmul(grad_up16, w_up.T)
    grad_middle_norm, grad_gain_mlp = norm_backward(grad_normed_two, unit_two, recip_two, gains[1])
    grad_middle = flat_cot + grad_middle_norm
    grad_middle16 = grad_middle.astype(jnp.bfloat16)
    grad_wmerge = matmul(mixed_heads.T, grad_middle16)
    grad_heads = matmul(grad_middle16, w_merge.T).astype(jnp.bfloat16).reshape(count_seqs, seq_len, H, HEAD)
    grad_queries, grad_keys, grad_values = attend_back(queries, key_rows, values, log_total, grad_heads)
    query16 = unrotate(grad_queries, cosine_table, sine_table).reshape(count_seqs * seq_len, H * HEAD).astype(jnp.bfloat16)
    key16 = unrotate(grad_keys, cosine_table, sine_table).reshape(count_seqs * seq_len, KV * HEAD).astype(jnp.bfloat16)
    value16 = grad_values.reshape(count_seqs * seq_len, KV * HEAD).astype(jnp.bfloat16)
    grad_wquery = matmul(normed_one.T, query16)
    grad_wkey = matmul(normed_one.T, key16)
    grad_wvalue = matmul(normed_one.T, value16)
    grad_normed_one = matmul(query16, w_query.T) + matmul(key16, w_key.T) + matmul(value16, w_value.T)
    grad_input_norm, grad_gain_attn = norm_backward(grad_normed_one, unit_one, recip_one, gains[0])
    input_grad = (grad_middle + grad_input_norm).reshape(cotangent.shape)
    return (input_grad, (grad_wquery, grad_wkey, grad_wvalue, grad_wmerge, grad_wgate, grad_wup, grad_wdown, grad_gain_attn, grad_gain_mlp))

def adamw_step(master, moments, grad, decay_rate, step_rate):
    first_moment = BETA_ONE * moments[0] + (1.0 - BETA_ONE) * grad
    second = BETA_TWO * moments[1] + (1.0 - BETA_TWO) * grad * grad
    update = first_moment / (1.0 - BETA_ONE ** STEP_COUNT) / (jnp.sqrt(second / (1.0 - BETA_TWO ** STEP_COUNT)) + ADAM_EPS)
    return (master - step_rate * (update + decay_rate * master), jnp.stack([first_moment, second]))

def reference(inputs, cotangent, w_query, w_key, w_value, w_merge, w_gate, w_up, w_down, gain_attn, gain_mlp, mom_query, mom_key, mom_value, mom_merge, mom_gate, mom_up, mom_down, mom_attn, mom_mlp):
    masters = (w_query, w_key, w_value, w_merge, w_gate, w_up, w_down, gain_attn, gain_mlp)
    moments = (mom_query, mom_key, mom_value, mom_merge, mom_gate, mom_up, mom_down, mom_attn, mom_mlp)
    weights = tuple((piece.astype(jnp.bfloat16) for piece in masters[:7]))
    gains = tuple((piece.astype(jnp.bfloat16) for piece in masters[7:]))
    cosine_table, sine_table = rotary_tables(SEQ_LEN, HEAD)
    block_seqs = math.gcd(SEQS, 16)
    block_count = SEQS // block_seqs
    blocked_in = inputs.reshape(block_count, block_seqs, SEQ_LEN, D)
    blocked_cot = cotangent.reshape(block_count, block_seqs, SEQ_LEN, D)

    def visit_block(totals, block_pair):
        output, saved = forward_pass(block_pair[0], weights, gains, cosine_table, sine_table)
        input_grad, partial_value = backward_pass(block_pair[1], saved, weights, gains, cosine_table, sine_table)
        return (tuple((left_side + right_side for left_side, right_side in zip(totals, partial_value))), (output, input_grad))
    zero_grads = tuple((jnp.zeros(piece.shape, jnp.float32) for piece in masters))
    totals, (outputs, input_grads) = lax.scan(visit_block, zero_grads, (blocked_in, blocked_cot))
    grad_scale = 1.0 / math.sqrt(TOKENS)
    grads = tuple((piece * grad_scale for piece in totals))
    decays = (WEIGHT_DECAY,) * 7 + (0.0, 0.0)
    rates = (LEARN_RATE,) * 7 + (GAIN_RATE, GAIN_RATE)
    results = [adamw_step(masters[index], moments[index], grads[index], decays[index], rates[index]) for index in range(9)]
    return (outputs.reshape(inputs.shape), input_grads.reshape(inputs.shape), grads[0], grads[1], grads[2], grads[3], grads[4], grads[5], grads[6], grads[7], grads[8], results[0][0], results[1][0], results[2][0], results[3][0], results[4][0], results[5][0], results[6][0], results[7][0], results[8][0], results[0][1], results[1][1], results[2][1], results[3][1], results[4][1], results[5][1], results[6][1], results[7][1], results[8][1])
```

```python
import math

import jax
import jax.numpy as jnp
import numpy as np
from jax import lax
from jax.experimental import pallas as pl
from jax.experimental.pallas import tpu as pltpu
from jax.sharding import PartitionSpec as P

H = 15
KV = 5
HEAD = 64
HALF = HEAD // 2
GROUP = 8
REPEAT = H // KV

EPS_NORM = 1e-05
THETA = 100000.0
BETA_ONE = 0.9
BETA_TWO = 0.95
ADAM_EPS = 1e-08
LEARN_RATE = 0.01
GAIN_RATE = 0.1
WEIGHT_DECAY = 0.1
STEP_COUNT = 3.0
NEG_LARGE = -1e30

AXES = ("replica", "shard")
F32 = jnp.float32
BF16 = jnp.bfloat16
INTERPRET = False


def dot_nn(a, b):
    return lax.dot_general(a, b, (((1,), (0,)), ((), ())), preferred_element_type=F32)


def dot_nt(a, b):
    return lax.dot_general(a, b, (((1,), (1,)), ((), ())), preferred_element_type=F32)


def dot_tn(a, b):
    return lax.dot_general(a, b, (((0,), (0,)), ((), ())), preferred_element_type=F32)


def shape(dims, kind):
    return jax.ShapeDtypeStruct(dims, kind)


def call(body, name, ins, outs, scratch=()):
    vmem = pl.BlockSpec(memory_space=pltpu.VMEM)
    smem = pl.BlockSpec(memory_space=pltpu.SMEM)
    return pl.pallas_call(
        body,
        name=name,
        out_shape=tuple(outs),
        in_specs=[smem] + [vmem] * (len(ins) - 1),
        out_specs=tuple(vmem for _ in outs),
        scratch_shapes=list(scratch),
        interpret=INTERPRET,
    )(*ins)


class Plane:
    def __init__(self):
        self.reps = lax.axis_size("replica")
        self.shards = lax.axis_size("shard")
        self.outer = self.reps // GROUP
        self.rank = lax.axis_index("replica") // self.outer
        self.shard = lax.axis_index("shard")
        self.groups = [[g * self.outer + o for o in range(self.outer)] for g in range(GROUP)]

    def swap(self, x, mask):
        pairs = []
        for g in range(GROUP):
            for o in range(self.outer):
                for s in range(self.shards):
                    src = (g * self.outer + o) * self.shards + s
                    dst = ((g ^ mask) * self.outer + o) * self.shards + s
                    pairs.append((src, dst))
        return lax.ppermute(x, AXES, pairs)

    def ring(self, x):
        n = self.shards
        return lax.ppermute(x, "shard", [(i, (i + 1) % n) for i in range(n)])

    def outer_gather(self, x, axis):
        if self.outer == 1:
            return x
        return lax.all_gather(x, "replica", axis=axis, tiled=True, axis_index_groups=self.groups)

    def outer_scatter(self, x, axis):
        if self.outer == 1:
            return x
        return lax.psum_scatter(
            x, "replica", scatter_dimension=axis, tiled=True, axis_index_groups=self.groups
        )

    def ring_gather(self, x):
        out = [x]
        for _ in range(self.shards - 1):
            out.append(self.ring(out[-1]))
        return out

    def ring_scatter(self, blocks):
        acc = blocks[1]
        for i in range(2, self.shards):
            acc = self.ring(acc) + blocks[i]
        return self.ring(acc), blocks[0]

    def gather(self, x):
        out = [None] * GROUP
        out[0] = x
        for m in (2, 4, 6):
            out[m] = self.swap(x, m)
        for m in (0, 2, 4, 6):
            out[m + 1] = self.swap(out[m], 1)
        return out

    def exchange(self, blocks):
        return [blocks[0]] + [self.swap(blocks[m], m) for m in range(1, GROUP)]

    def scatter(self, pos, even, odd, name):
        got = self.swap(odd, 1)
        dims = even.shape[1:]

        def add(pos_ref, even_ref, got_ref, *outs):
            for j in range(4):
                both = even_ref[j].astype(F32) + got_ref[j].astype(F32)
                outs[j][...] = both.astype(outs[j].dtype)

        kept, *sent = call(
            add, name, (pos, even, got), [shape(dims, F32)] + [shape(dims, BF16)] * 3
        )
        return [kept] + [self.swap(sent[j], 2 * (j + 1)) for j in (2, 0, 1)]

    def total(self, x):
        if self.outer > 1:
            return lax.psum(x, "replica")
        for m in (1, 2, 4):
            x = x + self.swap(x, m)
        return x


def adamw_core(master, first, second, grad, decay_rate, step_rate):
    first = BETA_ONE * first + (1.0 - BETA_ONE) * grad
    second = BETA_TWO * second + (1.0 - BETA_TWO) * grad * grad
    update = (
        first
        / (1.0 - BETA_ONE**STEP_COUNT)
        / (jnp.sqrt(second / (1.0 - BETA_TWO**STEP_COUNT)) + ADAM_EPS)
    )
    return master - step_rate * (update + decay_rate * master), first, second


def adamw_step(master, moments, grad, decay_rate, step_rate):
    new, first, second = adamw_core(
        master, moments[0], moments[1], grad, decay_rate, step_rate
    )
    return grad, new, jnp.stack([first, second])


def reciprocal_of(field):
    return lax.rsqrt(jnp.mean(field * field, axis=0, keepdims=True) + EPS_NORM)


def norm_back(grad_unit, field):
    reciprocal = reciprocal_of(field)
    unit = field * reciprocal
    return reciprocal * (grad_unit - unit * jnp.mean(grad_unit * unit, axis=0, keepdims=True))


def shards(
    inputs,
    cotangent,
    w_query,
    w_key,
    w_value,
    w_merge,
    w_gate,
    w_up,
    w_down,
    gain_attn,
    gain_mlp,
    *moments,
):
    masters = (w_query, w_key, w_value, w_merge, w_gate, w_up, w_down, gain_attn, gain_mlp)
    plane = Plane()
    num = plane.shards
    count_seqs, seq, width = inputs.shape
    assert count_seqs == 1
    pos = jnp.stack([plane.rank, plane.shard]).astype(jnp.int32)
    x_t = inputs.reshape(seq, width).T
    cot_t = cotangent.reshape(seq, width).T
    row_a = gain_attn.reshape(1, -1)
    row_m = gain_mlp.reshape(1, -1)
    part = width // num

    if plane.outer == 1:
        wq, wk, wv, wo, wg, wu, wd = masters[:7]
    else:
        wq, wk, wv, wo, wg, wu, wd = (
            plane.outer_gather(piece.astype(BF16), 1).astype(F32) for piece in masters[:7]
        )
    wk_t, wv_t, wg_t, wu_t, wd_t = wk.T, wv.T, wg.T, wu.T, wd.T
    qn, kn, ffn, ffo = wq.shape[1], wk.shape[1], wg.shape[1], wd.shape[0]
    hn = qn + 2 * kn
    on = wo.shape[1]
    token_count = seq * plane.reps * num
    grad_scale = 1.0 / math.sqrt(token_count)

    frequency = THETA ** (-2.0 * np.arange(HALF, dtype=np.float32) / HEAD)
    angles = frequency.astype(np.float32)[:, None] * np.arange(seq, dtype=np.float32)[None, :]
    cos_t = jnp.asarray(np.cos(angles), F32)
    sin_t = jnp.asarray(np.sin(angles), F32)

    def owner(s, i):
        return lax.rem(s - i + num, num)

    def rows_of(s, i):
        return pl.ds(pl.multiple_of(owner(s, i) * part, 16), part)

    def lanes(*pieces):
        return jnp.concatenate(pieces, axis=1)

    def rounded(value):
        return value.astype(BF16).astype(F32)

    def prep_attn(pos_ref, x_ref, wq_ref, wk_ref, wv_ref, gain_ref, unit_ref, qkv_ref):
        field = x_ref[...]
        unit_ref[...] = (field * reciprocal_of(field)).astype(BF16)
        gain = rounded(gain_ref[...])
        whole = jnp.concatenate([wq_ref[...].T, wk_ref[...], wv_ref[...]], axis=0)
        qkv_ref[...] = (rounded(whole) * gain).astype(BF16)

    unit1, qkv_own = call(
        prep_attn,
        "prep_attn",
        (pos, x_t, wq, wk_t, wv_t, row_a),
        [shape((width, seq), BF16), shape((hn, part), BF16)],
    )
    qkv_w = plane.ring_gather(qkv_own)
    all1 = plane.gather(unit1)

    def prep_mlp(
        pos_ref, cot_ref, wo_ref, wg_ref, wu_ref, wd_ref, gain_ref, dy_ref, o_ref, gu_ref, d_ref
    ):
        dy_ref[...] = cot_ref[...].astype(BF16)
        o_ref[...] = wo_ref[...].T.astype(BF16)
        gain = rounded(gain_ref[...])
        gu_ref[:ffn, :] = (rounded(wg_ref[...]) * gain).astype(BF16)
        gu_ref[ffn:, :] = (rounded(wu_ref[...]) * gain).astype(BF16)
        d_ref[...] = wd_ref[...].astype(BF16)

    dy, o_own, gu_own, d_own = call(
        prep_mlp,
        "prep_mlp",
        (pos, cot_t, wo, wg_t, wu_t, wd_t, row_m),
        [
            shape((width, seq), BF16),
            shape((on, part), BF16),
            shape((2 * ffn, part), BF16),
            shape((on, ffo), BF16),
        ],
    )
    o_ring = plane.ring_gather(o_own)
    gu_w = plane.ring_gather(gu_own)
    d_ring = plane.ring_gather(d_own)

    def project(pos_ref, *refs):
        units, weights, outs = refs[:8], refs[8 : 8 + num], refs[8 + num :]
        for j in range(4):
            acc = None
            for i in range(num):
                rows = rows_of(pos_ref[1], i)
                both = lanes(units[2 * j][rows, :], units[2 * j + 1][rows, :])
                term = dot_nn(weights[i][...], both)
                acc = term if acc is None else acc + term
            outs[2 * j][...] = acc[:, :seq].astype(BF16)
            outs[2 * j + 1][...] = acc[:, seq:].astype(BF16)

    mine = call(
        project, "project", (pos, *all1, *qkv_w), [shape((hn, seq), BF16)] * GROUP
    )
    heads = plane.exchange(mine)

    def stack_merge(pos_ref, *refs):
        out = refs[num]
        for i in range(num):
            out[owner(pos_ref[1], i)] = refs[i][...]

    (o_stack,) = call(
        stack_merge, "stack_merge", (pos, *o_ring), [shape((num, on, part), BF16)]
    )
    all_o = plane.gather(o_stack)

    def attend(pos_ref, *refs):
        pieces, cos_ref, sin_ref = refs[:8], refs[8], refs[9]
        mixed_ref, q_ref, k_ref, v_ref, p_ref, qf, kf, vf = refs[10:]
        for m in range(GROUP):
            col = pos_ref[0] ^ m
            piece = pieces[m][...].astype(F32)
            qf[pl.ds(pl.multiple_of(col * qn, 8), qn), :] = piece[:qn]
            kf[pl.ds(pl.multiple_of(col * kn, 8), kn), :] = piece[qn : qn + kn]
            vf[pl.ds(pl.multiple_of(col * kn, 8), kn), :] = piece[qn + kn :]
        cos, sin = cos_ref[...], sin_ref[...]

        def rope(src, dst, base):
            one = src[base : base + HALF, :]
            two = src[base + HALF : base + HEAD, :]
            dst[base : base + HALF, :] = (one * cos - two * sin).astype(BF16)
            dst[base + HALF : base + HEAD, :] = (two * cos + one * sin).astype(BF16)

        for h in range(H):
            rope(qf, q_ref, h * HEAD)
        for h in range(KV):
            rope(kf, k_ref, h * HEAD)
        v_ref[...] = vf[...].astype(BF16)
        key_pos = lax.broadcasted_iota(jnp.int32, (seq, REPEAT * seq), 0)
        query_pos = lax.broadcasted_iota(jnp.int32, (seq, REPEAT * seq), 1) % seq
        causal = key_pos <= query_pos
        for n in range(KV):
            top = n * REPEAT * HEAD
            query = lanes(
                *[q_ref[top + r * HEAD : top + (r + 1) * HEAD, :] for r in range(REPEAT)]
            )
            span = slice(n * HEAD, (n + 1) * HEAD)
            scores = dot_tn(k_ref[span, :], query) * (1.0 / math.sqrt(HEAD))
            scores = jnp.where(causal, scores, NEG_LARGE)
            probs = jnp.exp(scores - jnp.max(scores, axis=0, keepdims=True))
            probs = probs * (1.0 / jnp.sum(probs, axis=0, keepdims=True))
            p_ref[n] = probs
            mix = dot_nn(v_ref[span, :], probs.astype(BF16)).astype(BF16)
            for r in range(REPEAT):
                mixed_ref[top + r * HEAD : top + (r + 1) * HEAD, :] = mix[
                    :, r * seq : (r + 1) * seq
                ]

    mixed, q16, k16, v16, probs = call(
        attend,
        "attend",
        (pos, *heads, cos_t, sin_t),
        [
            shape((H * HEAD, seq), BF16),
            shape((H * HEAD, seq), BF16),
            shape((KV * HEAD, seq), BF16),
            shape((KV * HEAD, seq), BF16),
            shape((KV, seq, REPEAT * seq), F32),
        ],
        [
            pltpu.VMEM((H * HEAD, seq), F32),
            pltpu.VMEM((KV * HEAD, seq), F32),
            pltpu.VMEM((KV * HEAD, seq), F32),
        ],
    )

    def merge(pos_ref, *refs):
        weights, mixed_ref, x_ref, mid_ref, unit_ref = refs[:8], *refs[8:]
        for m in range(GROUP):
            acc = None
            for t in range(num):
                term = dot_nn(weights[m][t], mixed_ref[t * part : (t + 1) * part, :])
                acc = term if acc is None else acc + term
            mid_ref[pl.ds(pl.multiple_of((pos_ref[0] ^ m) * on, 8), on), :] = acc
        field = mid_ref[...] + x_ref[...]
        mid_ref[...] = field
        unit_ref[...] = (field * reciprocal_of(field)).astype(BF16)

    middle, unit2 = call(
        merge,
        "merge",
        (pos, *all_o, mixed, x_t),
        [shape((width, seq), F32), shape((width, seq), BF16)],
    )
    all2 = plane.gather(unit2)
    all_dy = plane.gather(dy)

    def split_down(pos_ref, *refs):
        outs, scr = refs[num : num + GROUP], refs[num + GROUP]
        per = GROUP // num
        for i in range(num):
            base = owner(pos_ref[1], i) * per
            for k in range(per):
                scr[base + k] = refs[i][:, k * ffn : (k + 1) * ffn]
        for m in range(GROUP):
            outs[m][...] = scr[pos_ref[0] ^ m]

    down_out = call(
        split_down,
        "split_down",
        (pos, *d_ring),
        [shape((on, ffn), BF16)] * GROUP,
        [pltpu.VMEM((GROUP, on, ffn), BF16)],
    )
    down_in = plane.exchange(down_out)

    def mlp(pos_ref, *refs):
        units, dys, weights, downs = refs[:8], refs[8:16], refs[16 : 16 + num], refs[16 + num : 24 + num]
        even_ref, odd_ref, hid_ref, dgu_ref, wd_ref, tall = refs[24 + num :]
        for m in range(GROUP):
            tall[pl.ds(pl.multiple_of((pos_ref[0] ^ m) * on, 8), on), :] = downs[m][...].astype(F32)
        wd_ref[...] = tall[...].astype(BF16)
        for j in range(4):
            cols = slice(j * 2 * seq, (j + 1) * 2 * seq)
            acc = None
            for i in range(num):
                rows = rows_of(pos_ref[1], i)
                both = lanes(units[2 * j][rows, :], units[2 * j + 1][rows, :])
                term = dot_nn(weights[i][...], both)
                acc = term if acc is None else acc + term
            d_hid = dot_tn(wd_ref[...], lanes(dys[2 * j][...], dys[2 * j + 1][...]))
            gate, up = acc[:ffn], acc[ffn:]
            sig = jax.nn.sigmoid(gate)
            hid_ref[:, cols] = (gate * sig * up).astype(BF16)
            d_gate = (d_hid * up * sig * (1.0 + gate * (1.0 - sig))).astype(BF16)
            d_up = (d_hid * gate * sig).astype(BF16)
            dgu_ref[:ffn, cols] = d_gate
            dgu_ref[ffn:, cols] = d_up
            for i in range(num):
                rows = rows_of(pos_ref[1], i)
                back = dot_tn(weights[i][...], dgu_ref[:, cols]).astype(BF16)
                even_ref[j, rows, :] = back[:, :seq]
                odd_ref[j, rows, :] = back[:, seq:]

    stack = shape((4, width, seq), BF16)
    even2, odd2, hidden, d_gu, down_w = call(
        mlp,
        "mlp",
        (pos, *all2, *all_dy, *gu_w, *down_in),
        [
            stack,
            stack,
            shape((ffn, GROUP * seq), BF16),
            shape((2 * ffn, GROUP * seq), BF16),
            shape((width, ffn), BF16),
        ],
        [pltpu.VMEM((width, ffn), F32)],
    )
    back2 = plane.scatter(pos, even2, odd2, "add_back2")

    def mlp_out(pos_ref, hid_ref, wd_ref, even_ref, odd_ref):
        for j in range(4):
            cols = slice(j * 2 * seq, (j + 1) * 2 * seq)
            out = dot_nn(wd_ref[...], hid_ref[:, cols]).astype(BF16)
            even_ref[j] = out[:, :seq]
            odd_ref[j] = out[:, seq:]

    even_y, odd_y = call(mlp_out, "mlp_out", (pos, hidden, down_w), [stack, stack])

    def mlp_grads(pos_ref, *refs):
        units, dys, hid_ref, dgu_ref = refs[:8], refs[8:16], refs[16], refs[17]
        gus, downs, tall = refs[18 : 18 + num], refs[18 + num : 26 + num], refs[26 + num]
        for i in range(num):
            rows = rows_of(pos_ref[1], i)
            both = lanes(*[unit[rows, :] for unit in units])
            gus[i][...] = dot_nt(dgu_ref[...], both).astype(BF16)
        tall[...] = dot_nt(lanes(*[d[...] for d in dys]), hid_ref[...])
        for m in range(GROUP):
            rows = pl.ds(pl.multiple_of((pos_ref[0] ^ m) * on, 8), on)
            downs[m][...] = tall[rows, :].astype(BF16)

    grads_mlp = call(
        mlp_grads,
        "mlp_grads",
        (pos, *all2, *all_dy, hidden, d_gu),
        [shape((2 * ffn, part), BF16)] * num + [shape((on, ffn), BF16)] * GROUP,
        [pltpu.VMEM((width, ffn), F32)],
    )
    gu_sum = plane.ring_scatter(grads_mlp[:num])
    d_back = plane.exchange(grads_mlp[num:])

    def join_down(pos_ref, *refs):
        outs, scr = refs[GROUP : GROUP + num], refs[GROUP + num]
        per = GROUP // num
        for m in range(GROUP):
            scr[pos_ref[0] ^ m] = refs[m][...]
        for i in range(num):
            base = owner(pos_ref[1], i) * per
            for k in range(per):
                outs[i][:, k * ffn : (k + 1) * ffn] = scr[base + k]

    d_blocks = call(
        join_down,
        "join_down",
        (pos, *d_back),
        [shape((on, ffo), BF16)] * num,
        [pltpu.VMEM((GROUP, on, ffn), BF16)],
    )
    d_sum = plane.ring_scatter(d_blocks)
    out_parts = plane.scatter(pos, even_y, odd_y, "add_out")

    def finish_out(pos_ref, mid_ref, a_ref, b_ref, c_ref, d_ref, out_ref):
        total = a_ref[...] + b_ref[...].astype(F32) + c_ref[...].astype(F32)
        out_ref[...] = mid_ref[...] + (total + d_ref[...].astype(F32))

    (out_t,) = call(
        finish_out, "finish_out", (pos, middle, *out_parts), [shape((width, seq), F32)]
    )

    def attend_back(pos_ref, *refs):
        parts, weights = refs[:4], refs[4:12]
        cot_ref, mid_ref, q_ref, k_ref, v_ref, p_ref, cos_ref, sin_ref = refs[12:20]
        dmid_ref, dmid16_ref = refs[20:22]
        outs = refs[22:30]
        dmix, dqf, dkf, dvf = refs[30:]
        back = parts[0][...]
        for piece in parts[1:]:
            back = back + piece[...].astype(F32)
        d_mid = cot_ref[...] + norm_back(back, mid_ref[...])
        dmid_ref[...] = d_mid
        dmid16_ref[...] = d_mid.astype(BF16)
        cols = [
            dmid_ref[pl.ds(pl.multiple_of((pos_ref[0] ^ m) * on, 8), on), :].astype(BF16)
            for m in range(GROUP)
        ]
        for t in range(num):
            acc = None
            for m in range(GROUP):
                term = dot_tn(weights[m][t], cols[m])
                acc = term if acc is None else acc + term
            dmix[t * part : (t + 1) * part, :] = acc.astype(BF16)
        cos, sin = cos_ref[...], sin_ref[...]

        def unrope(value, dst, base):
            one, two = value[:HALF], value[HALF:]
            dst[base : base + HALF, :] = one * cos + two * sin
            dst[base + HALF : base + HEAD, :] = two * cos - one * sin

        for n in range(KV):
            top = n * REPEAT * HEAD
            span = slice(n * HEAD, (n + 1) * HEAD)
            spans = [slice(top + r * HEAD, top + (r + 1) * HEAD) for r in range(REPEAT)]
            d_mix = lanes(*[dmix[sp, :] for sp in spans])
            query = lanes(*[q_ref[sp, :] for sp in spans])
            probs_n = p_ref[n]
            d_prob = dot_tn(v_ref[span, :], d_mix)
            inner = jnp.sum(probs_n * d_prob, axis=0, keepdims=True)
            d_score = (probs_n * (d_prob - inner) * (1.0 / math.sqrt(HEAD))).astype(BF16)
            d_query = dot_nn(k_ref[span, :], d_score)
            for r in range(REPEAT):
                unrope(d_query[:, r * seq : (r + 1) * seq], dqf, top + r * HEAD)
            unrope(dot_nt(query, d_score), dkf, n * HEAD)
            dvf[span, :] = dot_nt(d_mix, probs_n.astype(BF16))
        for m in range(GROUP):
            col = pos_ref[0] ^ m
            rows_q = pl.ds(pl.multiple_of(col * qn, 8), qn)
            rows_k = pl.ds(pl.multiple_of(col * kn, 8), kn)
            whole = jnp.concatenate([dqf[rows_q, :], dkf[rows_k, :], dvf[rows_k, :]], axis=0)
            outs[m][...] = whole.astype(BF16)

    d_middle, d_mid16, *d_mine = call(
        attend_back,
        "attend_back",
        (pos, *back2, *all_o, cot_t, middle, q16, k16, v16, probs, cos_t, sin_t),
        [shape((width, seq), F32), shape((width, seq), BF16)] + [shape((hn, seq), BF16)] * GROUP,
        [
            pltpu.VMEM((H * HEAD, seq), BF16),
            pltpu.VMEM((H * HEAD, seq), F32),
            pltpu.VMEM((KV * HEAD, seq), F32),
            pltpu.VMEM((KV * HEAD, seq), F32),
        ],
    )
    d_heads = plane.exchange(d_mine)

    def merge_grad(pos_ref, dmid_ref, mixed_ref, even_ref, odd_ref):
        for m in range(GROUP):
            rows = pl.ds(pl.multiple_of((pos_ref[0] ^ m) * on, 8), on)
            side = dmid_ref[rows, :].astype(BF16)
            dst = (even_ref, odd_ref)[m % 2]
            for t in range(num):
                dst[m // 2, t] = dot_nt(side, mixed_ref[t * part : (t + 1) * part, :]).astype(BF16)

    o_stacks = shape((4, num, on, part), BF16)
    even_o, odd_o = call(merge_grad, "merge_grad", (pos, d_middle, mixed), [o_stacks, o_stacks])
    o_parts = plane.scatter(pos, even_o, odd_o, "add_merge")

    def split_merge(pos_ref, *refs):
        outs, tall = refs[4 : 4 + num], refs[4 + num]
        total = refs[0][...]
        for ref in refs[1:4]:
            total = total + ref[...].astype(F32)
        tall[...] = total.astype(BF16)
        for i in range(num):
            outs[i][...] = tall[owner(pos_ref[1], i)]

    o_blocks = call(
        split_merge,
        "split_merge",
        (pos, *o_parts),
        [shape((on, part), BF16)] * num,
        [pltpu.VMEM((num, on, part), BF16)],
    )
    o_sum = plane.ring_scatter(o_blocks)

    def project_back(pos_ref, *refs):
        pieces, weights, even_ref, odd_ref = refs[:8], refs[8 : 8 + num], *refs[8 + num :]
        for j in range(4):
            both = lanes(pieces[2 * j][...], pieces[2 * j + 1][...])
            for i in range(num):
                rows = rows_of(pos_ref[1], i)
                back = dot_tn(weights[i][...], both).astype(BF16)
                even_ref[j, rows, :] = back[:, :seq]
                odd_ref[j, rows, :] = back[:, seq:]

    even1, odd1 = call(project_back, "project_back", (pos, *d_heads, *qkv_w), [stack, stack])
    back1 = plane.scatter(pos, even1, odd1, "add_back1")

    def project_grad(pos_ref, *refs):
        pieces, units, outs = refs[:8], refs[8:16], refs[16:]
        whole = lanes(*[piece[...] for piece in pieces])
        for i in range(num):
            rows = rows_of(pos_ref[1], i)
            outs[i][...] = dot_nt(whole, lanes(*[unit[rows, :] for unit in units])).astype(BF16)

    qkv_blocks = call(
        project_grad, "project_grad", (pos, *d_heads, *all1), [shape((hn, part), BF16)] * num
    )
    qkv_sum = plane.ring_scatter(qkv_blocks)

    def finish_grad(pos_ref, dmid_ref, x_ref, a_ref, b_ref, c_ref, d_ref, out_ref):
        back = a_ref[...] + b_ref[...].astype(F32) + c_ref[...].astype(F32)
        back = back + d_ref[...].astype(F32)
        out_ref[...] = dmid_ref[...] + norm_back(back, x_ref[...])

    (grad_t,) = call(
        finish_grad, "finish_grad", (pos, d_middle, x_t, *back1), [shape((width, seq), F32)]
    )

    sums = (qkv_sum, o_sum, gu_sum, d_sum)
    if plane.outer == 1:
        results, g_attn, g_mlp = update_fused(pos, sums, masters, moments, row_a, row_m, grad_scale)
    else:
        results, g_attn, g_mlp = update_plain(
            plane, sums, (wq, wk, wv, wg, wu), masters, moments, grad_scale
        )
    g_attn = plane.total(g_attn)
    g_mlp = plane.total(g_mlp)
    results = list(results) + [
        adamw_step(masters[7], moments[7], g_attn.reshape(-1), 0.0, GAIN_RATE),
        adamw_step(masters[8], moments[8], g_mlp.reshape(-1), 0.0, GAIN_RATE),
    ]
    return (
        (out_t.T.reshape(inputs.shape), grad_t.T.reshape(inputs.shape))
        + tuple(item[0] for item in results)
        + tuple(item[1] for item in results)
        + tuple(item[2] for item in results)
    )


def update_plain(plane, sums, weights, masters, moments, grad_scale):
    qkv, merged, gu, down = (a.astype(F32) + b.astype(F32) for a, b in sums)
    wq, wk, wv, wg, wu = weights
    gain_a = masters[7].astype(BF16).astype(F32)[None, :]
    gain_m = masters[8].astype(BF16).astype(F32)[None, :]
    qn, kn, ffn = wq.shape[1], wk.shape[1], wg.shape[1]
    qkv, gu, merged, down = qkv * grad_scale, gu * grad_scale, merged * grad_scale, down * grad_scale
    g_attn = jnp.sum(jnp.concatenate([wq, wk, wv], axis=1).T * qkv, axis=0, keepdims=True)
    g_mlp = jnp.sum(jnp.concatenate([wg, wu], axis=1).T * gu, axis=0, keepdims=True)
    qkv, gu = qkv * gain_a, gu * gain_m
    pieces = (
        qkv[:qn], qkv[qn : qn + kn], qkv[qn + kn :], merged, gu[:ffn], gu[ffn:], down,
    )
    results = [
        adamw_step(
            masters[i], moments[i], plane.outer_scatter(pieces[i].T, 1), WEIGHT_DECAY, LEARN_RATE
        )
        for i in range(7)
    ]
    return results, g_attn, g_mlp


def update_fused(pos, sums, masters, moments, row_a, row_m, grad_scale):
    def turned(x):
        return jnp.swapaxes(x, -1, -2)

    def step(w_ref, m_ref, grad, g_out, w_out, m_out):
        new, first, second = adamw_core(
            w_ref[...], m_ref[0], m_ref[1], grad, WEIGHT_DECAY, LEARN_RATE
        )
        g_out[...] = grad
        w_out[...] = new
        m_out[0] = first
        m_out[1] = second

    def summed(a_ref, b_ref):
        return (a_ref[...].astype(F32) + b_ref[...].astype(F32)) * grad_scale

    def half(ref):
        return ref[...].astype(BF16).astype(F32)

    def outs_of(w, m):
        return [shape(w.shape, F32), shape(w.shape, F32), shape(m.shape, F32)]

    wq, wk, wv, wo, wg, wu, wd = masters[:7]
    mq, mk, mv, mo, mg, mu, md = moments[:7]
    wk, wv, wg, wu, wd, mk, mv, mg, mu, md = (
        turned(item) for item in (wk, wv, wg, wu, wd, mk, mv, mg, mu, md)
    )
    qn, kn, ffn = wq.shape[1], wk.shape[0], wg.shape[0]
    row = shape(row_a.shape, F32)

    def update_qkv(pos_ref, a, b, wq_r, wk_r, wv_r, mq_r, mk_r, mv_r, gain, *outs):
        total = summed(a, b)
        whole = jnp.concatenate([wq_r[...].T, wk_r[...], wv_r[...]], axis=0)
        whole = whole.astype(BF16).astype(F32)
        outs[9][...] = jnp.sum(whole * total, axis=0, keepdims=True)
        grad = total * half(gain)
        step(wq_r, mq_r, grad[:qn].T, *outs[:3])
        step(wk_r, mk_r, grad[qn : qn + kn], *outs[3:6])
        step(wv_r, mv_r, grad[qn + kn :], *outs[6:9])

    qkv = call(
        update_qkv,
        "update_qkv",
        (pos, *sums[0], wq, wk, wv, mq, mk, mv, row_a),
        outs_of(wq, mq) + outs_of(wk, mk) + outs_of(wv, mv) + [row],
    )

    def update_merge(pos_ref, a, b, w_r, m_r, *outs):
        step(w_r, m_r, summed(a, b).T, *outs)

    merged = call(update_merge, "update_merge", (pos, *sums[1], wo, mo), outs_of(wo, mo))

    def update_gu(pos_ref, a, b, wg_r, wu_r, mg_r, mu_r, gain, *outs):
        total = summed(a, b)
        low, high = total[:ffn], total[ffn:]
        outs[6][...] = jnp.sum(half(wg_r) * low + half(wu_r) * high, axis=0, keepdims=True)
        gains = half(gain)
        step(wg_r, mg_r, low * gains, *outs[:3])
        step(wu_r, mu_r, high * gains, *outs[3:6])

    gu = call(
        update_gu,
        "update_gu",
        (pos, *sums[2], wg, wu, mg, mu, row_m),
        outs_of(wg, mg) + outs_of(wu, mu) + [row],
    )

    def update_down(pos_ref, a, b, w_r, m_r, *outs):
        step(w_r, m_r, summed(a, b), *outs)

    down = call(update_down, "update_down", (pos, *sums[3], wd, md), outs_of(wd, md))
    flip = [qkv[3:6], qkv[6:9], gu[:3], gu[3:6], down]
    flip = [tuple(turned(item) for item in group) for group in flip]
    results = [tuple(qkv[:3]), flip[0], flip[1], tuple(merged), flip[2], flip[3], flip[4]]
    return results, qkv[9], gu[6]


def solution(mesh):
    act = P(AXES, None, None)
    mat = P("shard", "replica")
    vec = P("shard")
    mom = P(None, "shard", "replica")
    momv = P(None, "shard")
    return jax.shard_map(
        shards,
        mesh=mesh,
        in_specs=(act,) * 2 + (mat,) * 7 + (vec,) * 2 + (mom,) * 7 + (momv,) * 2,
        out_specs=(act,) * 2 + ((mat,) * 7 + (vec,) * 2) * 2 + (mom,) * 7 + (momv,) * 2,
        check_vma=False,
    )
```
